256 devices in a mesh: expert: 32 (over z, y), edata: 8 (over x, core).
Axes of the slice: x: 4, y: 4, z: 8, core: 2. Of those that a mesh axis runs over, the one named last changes fastest.
Arguments:
- tokens: bfloat16 [8192, 2048], P(('expert', 'edata')), may hold values from -6 to 6
- out_grad: bfloat16 [8192, 2048], P(('expert', 'edata')), may hold values from -6 to 6
- routes: int32 [8192, 8], P(('expert', 'edata')), may hold values from 0 to 31, as said below
- gate_codes: int32 [8192, 8], P(('expert', 'edata')), may hold values from 1 to 4095
- w_gate: bfloat16 [32, 2048, 768], P('expert'), may hold values from -0.125 to 0.125
- w_up: bfloat16 [32, 2048, 768], P('expert'), may hold values from -0.125 to 0.125
- w_down: bfloat16 [32, 768, 2048], P('expert'), may hold values from -0.21875 to 0.21875
Outputs:
- mixed: bfloat16 [8192, 2048], P(('expert', 'edata'))
- input_grad: bfloat16 [8192, 2048], P(('expert', 'edata'))
- grad_down: float32 [2048, 32, 768], P('edata', 'expert')
The draws below stay inside these ranges and needn't reach their ends.
Inputs may be any that keep to these rules, and one draw needn't show every extreme that they name: `routes`: each token names 8 different experts. For each index of edata one expert, drawn anew in each draw, is named by exactly 16 of the 32 tokens of every device of that index of edata; any other expert is named by at most (8) tokens of one device.
All inputs are finite; a program needn't handle non-finite values.
Results may differ from the reference program's by a relative error of at most 0.017.
Values may be sent and summed in bfloat16 or wider, within the bound.
A program may use at most 128 MiB of HBM per device.

```python
import jax
import jax.numpy as jnp
from jax import lax

D = 2048
HID = 768
TOPK = 8
TOK_DEV = 32
BLOCK = 128
EXPERTS = 32
CAP = 16
TOKENS = 8192
N_EDATA = 8


def route_block(block_key, hot_expert):
    perm_key, pick_key, turn_key = jax.random.split(block_key, 3)
    ordering = jax.random.permutation(perm_key, EXPERTS).astype(jnp.int32)
    hot_last = jnp.argsort((ordering == hot_expert).astype(jnp.int32), stable=True)
    others = ordering[hot_last][:EXPERTS - 1]
    chosen = jax.random.permutation(pick_key, TOK_DEV).astype(jnp.int32) < CAP
    takes_hot = chosen.astype(jnp.int32)
    lengths = TOPK - takes_hot
    starts = jnp.cumsum(lengths) - lengths
    columns = jnp.arange(TOPK, dtype=jnp.int32)
    placing = (starts[:, None] + columns[None, :] - takes_hot[:, None]) % (EXPERTS - 1)
    picked = others[placing]
    row_set = jnp.where((columns[None, :] == 0) & chosen[:, None], hot_expert, picked)
    turn_by = jax.random.randint(turn_key, (TOK_DEV,), 0, TOPK).astype(jnp.int32)
    rolled = (columns[None, :] + turn_by[:, None]) % TOPK
    return jnp.take_along_axis(row_set, rolled, axis=1).astype(jnp.int32)


def draw_routes(key, part):
    blocks = TOKENS // TOK_DEV
    hot_all = jax.random.randint(jax.random.fold_in(key, 11), (N_EDATA,), 0, EXPERTS).astype(jnp.int32)
    block_ids = jnp.arange(blocks, dtype=jnp.int32)
    hot_of_block = hot_all[block_ids % N_EDATA]
    block_keys = jax.vmap(lambda block_index: jax.random.fold_in(key, block_index + 100))(block_ids)
    return jax.vmap(route_block)(block_keys, hot_of_block).reshape(TOKENS, TOPK)


def touch_ends(array, stream_key, least, top_value):
    place = [jax.random.randint(jax.random.fold_in(stream_key, axis), (), 0, length) for axis, length in enumerate(array.shape)]
    main_axis = array.shape.index(max(array.shape))
    beside = place[:main_axis] + [(place[main_axis] + 1) % array.shape[main_axis]] + place[main_axis + 1:]
    return array.at[tuple(place)].set(least).at[tuple(beside)].set(top_value)


def shard_levels(own_key, dims, pieces, low, largest):
    factor_of, own = 1.0, jax.random.fold_in(own_key, 6)
    for axis_at, shards_of in pieces:
        steps = jnp.exp(jax.random.uniform(jax.random.fold_in(own, axis_at), (shards_of,), jnp.float32, low / len(pieces), largest / len(pieces)))
        factor_of = factor_of * jnp.repeat(steps, dims[axis_at] // shards_of).reshape([-1 if axis == axis_at else 1 for axis in range(len(dims))])
    return factor_of


def scatter_about(key, extent, deviation, reach, shards=(), kind=jnp.bfloat16):
    gain = shard_levels(key, extent, shards, -0.22, 0.18) if shards else 1.0
    values = jax.random.normal(key, extent, jnp.float32) * deviation * gain
    return jnp.minimum(jnp.maximum(values, -reach), reach).astype(kind)


def setup_inputs(seed: int = 0) -> dict:
    key_of = jax.random.split(jax.random.key(seed), 8)
    tokens = scatter_about(key_of[0], (TOKENS, D), 1.0, 6.0, ((0, 256),))
    out_grad = scatter_about(key_of[1], (TOKENS, D), 1.0, 6.0, ((0, 256),))
    routes = draw_routes(jax.random.fold_in(key_of[7], 71), 0)
    gate_codes = touch_ends(jax.random.randint(key_of[3], (TOKENS, TOPK), 1, 4096), jax.random.fold_in(key_of[3], 1), 1, 4095).astype(jnp.int32)
    w_gate = scatter_about(key_of[4], (EXPERTS, D, HID), D ** -0.5, 0.125, ((0, 32),))
    w_up = scatter_about(key_of[5], (EXPERTS, D, HID), D ** -0.5, 0.125, ((0, 32),))
    w_down = scatter_about(key_of[6], (EXPERTS, HID, D), HID ** -0.5, 0.21875, ((0, 32),))
    return dict(tokens=tokens, out_grad=out_grad, routes=routes, gate_codes=gate_codes, w_gate=w_gate, w_up=w_up, w_down=w_down)


def take_rows(source, row_ids, row_limit):
    is_valid = row_ids < row_limit
    safe_rows = jnp.minimum(row_ids, row_limit - 1).astype(jnp.int32)
    return jnp.where(is_valid[:, None], jnp.take(source, safe_rows, axis=0), jnp.zeros((), source.dtype))


def expert_block(rows_in, grads_in, gate_mat, up_mat, down_mat):
    gate_pre = jnp.dot(rows_in, gate_mat, preferred_element_type=jnp.float32)
    up_pre = jnp.dot(rows_in, up_mat, preferred_element_type=jnp.float32)
    sig_gate = jax.nn.sigmoid(gate_pre)
    act_gate = gate_pre * sig_gate
    hidden_act = (act_gate * up_pre).astype(jnp.bfloat16)
    expert_out = jnp.dot(hidden_act, down_mat, preferred_element_type=jnp.float32).astype(jnp.bfloat16)
    grad_hidden = jnp.dot(grads_in, down_mat.T, preferred_element_type=jnp.float32)
    grad_gate_pre = (grad_hidden * up_pre * sig_gate * (1.0 + gate_pre * (1.0 - sig_gate))).astype(jnp.bfloat16)
    grad_up_pre = (grad_hidden * act_gate).astype(jnp.bfloat16)
    grad_rows = (jnp.dot(grad_gate_pre, gate_mat.T, preferred_element_type=jnp.float32)
                 + jnp.dot(grad_up_pre, up_mat.T, preferred_element_type=jnp.float32)).astype(jnp.bfloat16)
    return expert_out, grad_rows, hidden_act


def add_expert(total_grad, term, expert_id):
    current = lax.dynamic_index_in_dim(total_grad, expert_id, 0, keepdims=False)
    return lax.dynamic_update_index_in_dim(total_grad, current + term, expert_id, 0)


def reference(tokens, out_grad, routes, gate_codes, w_gate, w_up, w_down):
    routed = TOKENS * TOPK
    gate_float = gate_codes.astype(jnp.float32)
    gate_values = gate_float / jnp.sum(gate_float, axis=1, keepdims=True)
    scaled = (gate_values[:, :, None] * out_grad[:, None, :].astype(jnp.float32)).astype(jnp.bfloat16).reshape(routed, D)
    flat_expert = routes.reshape(routed).astype(jnp.int32)
    expert_ids = jnp.arange(EXPERTS, dtype=jnp.int32)
    counts = jnp.sum((flat_expert[:, None] == expert_ids[None, :]).astype(jnp.int32), axis=0)
    padded = (counts + BLOCK - 1) // BLOCK * BLOCK
    begins = jnp.cumsum(padded) - padded
    firsts = jnp.cumsum(counts) - counts
    sorted_order = jnp.argsort(flat_expert, stable=True).astype(jnp.int32)
    sorted_expert = flat_expert[sorted_order]
    place_sorted = (begins[sorted_expert] + jnp.arange(routed, dtype=jnp.int32) - firsts[sorted_expert]).astype(jnp.int32)
    block_count = routed // BLOCK + EXPERTS
    slot_total = block_count * BLOCK
    source_of = jnp.full((slot_total,), routed, jnp.int32).at[place_sorted].set(sorted_order)
    place_of = jnp.zeros((routed,), jnp.int32).at[sorted_order].set(place_sorted)
    block_starts = jnp.arange(block_count, dtype=jnp.int32) * BLOCK
    block_expert = jnp.clip(jnp.sum((begins[None, :] <= block_starts[:, None]).astype(jnp.int32), axis=1) - 1, 0, EXPERTS - 1).astype(jnp.int32)
    token_of = jnp.where(source_of < routed, source_of // TOPK, TOKENS).astype(jnp.int32)

    def block_step(sum_down, block_input):
        row_ids, token_ids, expert_id = block_input
        rows_in = take_rows(tokens, token_ids, TOKENS)
        grads_in = take_rows(scaled, row_ids, routed)
        gate_mat = lax.dynamic_index_in_dim(w_gate, expert_id, 0, keepdims=False)
        up_mat = lax.dynamic_index_in_dim(w_up, expert_id, 0, keepdims=False)
        down_mat = lax.dynamic_index_in_dim(w_down, expert_id, 0, keepdims=False)
        expert_out, grad_rows, hidden_act = expert_block(rows_in, grads_in, gate_mat, up_mat, down_mat)
        sum_down = add_expert(sum_down, jnp.dot(grads_in.T, hidden_act, preferred_element_type=jnp.float32), expert_id)
        return sum_down, (expert_out, grad_rows)

    zero_grad = jnp.zeros((EXPERTS, D, HID), jnp.float32)
    sum_down, outputs = lax.scan(block_step, zero_grad,
                                 (source_of.reshape(block_count, BLOCK), token_of.reshape(block_count, BLOCK), block_expert))
    out_flat = outputs[0].reshape(slot_total, D)
    grad_flat = outputs[1].reshape(slot_total, D)
    rows_out = jnp.take(out_flat, place_of, axis=0).reshape(TOKENS, TOPK, D)
    rows_grad = jnp.take(grad_flat, place_of, axis=0).reshape(TOKENS, TOPK, D)
    mixed = jnp.sum(gate_values[:, :, None] * rows_out.astype(jnp.float32), axis=1).astype(jnp.bfloat16)
    input_grad = jnp.sum(rows_grad.astype(jnp.float32), axis=1).astype(jnp.bfloat16)
    grad_down = jnp.transpose(sum_down, (1, 0, 2))
    return (mixed, input_grad, grad_down)
```

```python
import functools

import jax
import jax.numpy as jnp
from jax import lax
from jax.experimental import pallas as pl
from jax.experimental.pallas import tpu as pltpu
from jax.sharding import PartitionSpec as P

MESH = pl.DeviceIdType.MESH
NZ = 8
NY = 4
SLOTS = 8
F32 = jnp.float32
BF16 = jnp.bfloat16


def position():
    me = lax.axis_index("expert")
    return me // NY, lax.rem(me, NY)


def at_z(z, y, step):
    return lax.rem(z + step + NZ, NZ) * NY + y


def at_y(z, y, step):
    return z * NY + lax.rem(y + step + NY, NY)


def greet(z, y):
    barrier = pltpu.get_barrier_semaphore()
    peers = [at_z(z, y, 1), at_z(z, y, -1)] + [at_y(z, y, j) for j in range(1, NY)]
    for peer in peers:
        pl.semaphore_signal(
            barrier, inc=1, device_id={"expert": peer}, device_id_type=MESH
        )
    pl.semaphore_wait(barrier, len(peers))


def remote(src, dst, send_sem, recv_sem, peer):
    return pltpu.make_async_remote_copy(
        src_ref=src,
        dst_ref=dst,
        send_sem=send_sem,
        recv_sem=recv_sem,
        device_id={"expert": peer},
        device_id_type=MESH,
    )


def ranks_of(gates):
    lanes = gates.shape[1]
    earlier = lax.broadcasted_iota(jnp.int32, (lanes, lanes), 0) < lax.broadcasted_iota(
        jnp.int32, (lanes, lanes), 1
    )
    return jnp.dot(
        (gates > 0).astype(BF16), earlier.astype(BF16), preferred_element_type=F32
    )


def pick_rows(gates_ref, ranks_ref, z, y, tok_rows):
    slot = lax.broadcasted_iota(jnp.int32, (SLOTS, gates_ref.shape[1]), 0).astype(F32)
    picks, weights = [], []
    for j, base in [(j, 0.0) for j in range(NY)] + [(0, float(SLOTS))]:
        expert = at_y(z, y, j)
        gate_row = gates_ref[pl.ds(expert, 1), :]
        rank_row = ranks_ref[pl.ds(expert, 1), :]
        weight = jnp.where(rank_row == slot + base, gate_row, 0.0)
        picks.append(jnp.where(weight > 0, 1.0, 0.0))
        weights.append(jnp.sum(weight, axis=1, keepdims=True))
    picked = jnp.concatenate(picks, axis=0)[:, :tok_rows].astype(BF16)
    return picked, jnp.concatenate(weights, axis=0)


def pick_overflow(gates, ranks, tok_rows):
    rows = [
        jnp.sum(jnp.where(ranks == float(SLOTS + s), gates, 0.0), axis=0, keepdims=True)
        for s in range(SLOTS)
    ]
    weight = jnp.concatenate(rows, axis=0)
    picked = jnp.where(weight > 0, 1.0, 0.0)[:, :tok_rows].astype(BF16)
    return picked, jnp.sum(weight, axis=1, keepdims=True)


def dispatch_kernel(
    x_ref, d_ref, routes_ref, codes_ref,
    rx, rd, vx, vd, gt, flag,
    xg, dg, sx, sd, own, ranks,
    ring_send, ring_recv, y_send, y_recv, v_send, v_recv,
):
    z, y = position()
    tok_rows = x_ref.shape[0]
    experts = gt.shape[1]
    routes = routes_ref[...]
    codes = codes_ref[...].astype(F32)
    gates = codes / jnp.sum(codes, axis=0, keepdims=True)
    expert_ids = lax.broadcasted_iota(jnp.int32, (experts, routes.shape[1]), 0)
    table = jnp.zeros(expert_ids.shape, F32)
    for k in range(routes.shape[0]):
        table = table + jnp.where(
            routes[k : k + 1, :] == expert_ids, gates[k : k + 1, :], 0.0
        )
    gt[0] = table
    greet(z, y)

    right, left = at_z(z, y, 1), at_z(z, y, -1)
    three = pl.ds(1, NY - 1)

    def block(item, r):
        if item == 0:
            return x_ref if r == 0 else xg.at[r]
        if item == 1:
            return d_ref if r == 0 else dg.at[r]
        if item == 2:
            return gt.at[r]
        return (vx if item == 3 else vd).at[r, three]

    half = NZ // 2
    rights, lefts = {}, {}
    for item in range(5):
        long_right = item in (0, 2, 3)
        for s in range(half if long_right else half - 1):
            rights[item, s] = remote(
                block(item, s), block(item, s + 1),
                ring_send.at[item, s], ring_recv.at[item, s + 1], right,
            )
        for s in range(half - 1 if long_right else half):
            r = (NZ - s) % NZ
            lefts[item, s] = remote(
                block(item, r), block(item, NZ - 1 - s),
                ring_send.at[item, half + s], ring_recv.at[item, NZ - 1 - s], left,
            )

    def forward(items, s):
        for item in items:
            for way in (rights, lefts):
                if (item, s) in way:
                    way[item, s].start()

    def arrive(items, s):
        for item in items:
            for way in (rights, lefts):
                if (item, s - 1) in way:
                    way[item, s - 1].wait_recv()

    forward((0, 2, 1), 0)

    rank_own = ranks_of(table)
    ranks[0] = rank_own
    picked, weight = pick_overflow(table, rank_own, tok_rows)
    own[0] = jnp.dot(picked, x_ref[...], preferred_element_type=F32).astype(BF16)
    own[1] = (
        jnp.dot(picked, d_ref[...], preferred_element_type=F32) * weight
    ).astype(BF16)
    v_copies = []
    for j in range(1, NY):
        for i, dst in ((0, vx), (1, vd)):
            copy = remote(
                own.at[i], dst.at[0, j], v_send.at[i, j], v_recv.at[i, j], at_y(z, y, j)
            )
            copy.start()
            v_copies.append(copy)
    mine = table * jnp.where(expert_ids == z * NY + y, 1.0, 0.0)
    count = jnp.sum(jnp.where(mine > 0, 1.0, 0.0))
    flag[...] = jnp.full(flag.shape, count, F32)

    y_copies = []

    def select(r):
        if r:
            ranks[r] = ranks_of(gt[r])
        picked, weight = pick_rows(gt.at[r], ranks.at[r], z, y, tok_rows)
        got_x = jnp.dot(picked, block(0, r)[...], preferred_element_type=F32)
        got_d = jnp.dot(picked, block(1, r)[...], preferred_element_type=F32) * weight
        for i, got, near, over, out in ((0, got_x, rx, vx, sx), (1, got_d, rd, vd, sd)):
            for j in range(1, NY):
                out[r, j] = got[SLOTS * j : SLOTS * (j + 1)].astype(BF16)
                copy = remote(
                    out.at[r, j], near.at[r, j],
                    y_send.at[i, r, j], y_recv.at[i, r, j], at_y(z, y, j),
                )
                copy.start()
                y_copies.append(copy)
            near[r, 0] = got[:SLOTS].astype(BF16)
            over[r, 0] = got[SLOTS * NY :].astype(BF16)

    select(0)
    for copy in v_copies:
        copy.wait_recv()
    forward((3, 4), 0)
    for s in range(1, half):
        arrive((0, 2, 1), s)
        forward((0, 2, 1), s)
        select(s)
        select(NZ - s)
        arrive((3, 4), s)
        forward((3, 4), s)
    arrive((0, 2, 1), half)
    select(half)
    arrive((3, 4), half)
    for copy in y_copies:
        copy.wait_recv()
    for copy in v_copies + y_copies + list(rights.values()) + list(lefts.values()):
        copy.wait_send()


def return_kernel(
    eo, ed, vo, vd, gt,
    mixed, grad,
    bo, bd, part, part_send, over, over_send, last, ranks,
    y_send, y_recv, ring_send, ring_recv, v_send, v_recv,
):
    z, y = position()
    tok_rows = mixed.shape[0]
    half = NZ // 2
    right, left = at_z(z, y, 1), at_z(z, y, -1)
    greet(z, y)
    y_copies = {}
    order = [half]
    for s in range(1, half):
        order += [half + s, half - s]
    order.append(0)
    for r in order:
        for i, src, dst in ((0, eo, bo), (1, ed, bd)):
            for j in range(1, NY):
                copy = remote(
                    src.at[r, j], dst.at[r, j],
                    y_send.at[i, r, j], y_recv.at[i, r, j], at_y(z, y, -j),
                )
                copy.start()
                y_copies[i, r, j] = copy
    for r in range(NZ):
        ranks[r] = ranks_of(gt[r])

    def gathered(i, r):
        picked, weight = pick_rows(gt.at[r], ranks.at[r], z, y, tok_rows)
        back, here, spill = ((bo, eo, vo), (bd, ed, vd))[i]
        for j in range(1, NY):
            y_copies[i, r, j].wait_recv()
        rows = jnp.concatenate(
            [here[r, 0].astype(F32)]
            + [back[r, j].astype(F32) for j in range(1, NY)]
            + [spill[r, 0].astype(F32)],
            axis=0,
        )
        if i == 0:
            rows = rows * weight
        return lax.dot_general(
            picked, rows.astype(BF16), (((0,), (0,)), ((), ())), preferred_element_type=F32
        )

    chains = {
        (0, -1): list(range(half, 0, -1)),
        (0, 1): list(range(half + 1, NZ)),
        (1, -1): list(range(half - 1, 0, -1)),
        (1, 1): list(range(half, NZ)),
    }
    ring, spills = {}, {}
    for (i, way), places in chains.items():
        w = 0 if way < 0 else 1
        peer = left if way < 0 else right
        for r in places:
            to = r + way
            ring[i, way, r] = remote(
                part_send.at[i, w, r], part.at[i, w, to],
                ring_send.at[0, i, w, r], ring_recv.at[0, i, w, to], peer,
            )
            spills[i, way, r] = remote(
                over_send.at[i, w, r], over.at[i, w, to],
                ring_send.at[1, i, w, r], ring_recv.at[1, i, w, to], peer,
            )
    landing = {-1: 0, 1: NZ}
    for s in range(half):
        for (i, way), places in chains.items():
            if s >= len(places):
                continue
            r = places[s]
            w = 0 if way < 0 else 1
            spill = (vo, vd)[i][r, pl.ds(1, NY - 1)]
            if s:
                spills[i, way, places[s - 1]].wait_recv()
                spill = (spill.astype(F32) + over[i, w, r].astype(F32)).astype(BF16)
            over_send[i, w, r] = spill
            spills[i, way, r].start()
            total = gathered(i, r)
            if s:
                ring[i, way, places[s - 1]].wait_recv()
                total = total + part[i, w, r].astype(F32)
            part_send[i, w, r] = total.astype(BF16)
            ring[i, way, r].start()
    totals = [gathered(i, 0) for i in range(2)]
    v_copies = []
    for i in range(2):
        spill = (vo, vd)[i][0, pl.ds(1, NY - 1)].astype(F32)
        for way in (-1, 1):
            spills[i, way, chains[i, way][-1]].wait_recv()
            spill = spill + over[i, 0 if way < 0 else 1, landing[way]].astype(F32)
        over_send[i, 0, 0] = spill.astype(BF16)
        for j in range(1, NY):
            copy = remote(
                over_send.at[i, 0, 0, j - 1], last.at[i, j],
                v_send.at[i, j], v_recv.at[i, j], at_y(z, y, -j),
            )
            copy.start()
            v_copies.append(copy)
    picked, weight = pick_overflow(gt[0], ranks[0], tok_rows)
    for copy in v_copies:
        copy.wait_recv()
    for i, out in ((0, mixed), (1, grad)):
        rows = last[i, 1].astype(F32)
        for j in range(2, NY):
            rows = rows + last[i, j].astype(F32)
        if i == 0:
            rows = rows * weight
        total = totals[i] + lax.dot_general(
            picked, rows.astype(BF16), (((0,), (0,)), ((), ())), preferred_element_type=F32
        )
        for way in (-1, 1):
            ring[i, way, chains[i, way][-1]].wait_recv()
            total = total + part[i, 0 if way < 0 else 1, landing[way]].astype(F32)
        out[...] = total.astype(BF16)
    for copy in (
        list(y_copies.values()) + list(ring.values()) + list(spills.values()) + v_copies
    ):
        copy.wait_send()


def expert_kernel(
    flag, x_ref, d_ref, vx_ref, vd_ref, wg, wu, wd,
    eo, ed, vo, vd, gd,
    acc_o, acc_d, acc_w,
):
    step = pl.program_id(0)
    last = pl.num_programs(0) - 1
    rows = x_ref.shape[0]
    is_hot = flag[0] > float(SLOTS)
    over_cols = (((1,), (1,)), ((), ()))
    over_rows = (((0,), (0,)), ((), ()))

    def part(at, rows_in, grads_in):
        span = pl.ds(at * rows, rows)
        gate_pre = jnp.dot(rows_in[...], wg[...], preferred_element_type=F32)
        up_pre = jnp.dot(rows_in[...], wu[...], preferred_element_type=F32)
        sig = jax.nn.sigmoid(gate_pre)
        act = gate_pre * sig
        hidden = (act * up_pre).astype(BF16)
        out = jnp.dot(hidden, wd[...], preferred_element_type=F32)
        grad_hidden = lax.dot_general(
            grads_in[...], wd[...], over_cols, preferred_element_type=F32
        )
        grad_gate = (grad_hidden * up_pre * sig * (1.0 + gate_pre * (1.0 - sig))).astype(BF16)
        grad_up = (grad_hidden * act).astype(BF16)
        back = lax.dot_general(grad_gate, wg[...], over_cols, preferred_element_type=F32)
        back = back + lax.dot_general(grad_up, wu[...], over_cols, preferred_element_type=F32)

        @pl.when(step == 0)
        def _():
            acc_o[span, :] = out
            acc_d[span, :] = back

        @pl.when(step > 0)
        def _():
            acc_o[span, :] += out
            acc_d[span, :] += back

        return lax.dot_general(grads_in[...], hidden, over_rows, preferred_element_type=F32)

    acc_w[...] = part(0, x_ref, d_ref)

    @pl.when(is_hot)
    def _():
        acc_w[...] += part(1, vx_ref, vd_ref)

    gd[...] = acc_w[...].astype(BF16)

    @pl.when(step == last)
    def _():
        eo[...] = acc_o[:rows, :].astype(BF16)
        ed[...] = acc_d[:rows, :].astype(BF16)

    @pl.when(jnp.logical_and(step == last, is_hot))
    def _():
        vo[...] = acc_o[rows:, :].astype(BF16)
        vd[...] = acc_d[rows:, :].astype(BF16)

    @pl.when(jnp.logical_and(step == last, jnp.logical_not(is_hot)))
    def _():
        vo[...] = jnp.zeros_like(vo)
        vd[...] = jnp.zeros_like(vd)


def shards(tokens, out_grad, routes, gate_codes, w_gate, w_up, w_down):
    tok_rows, width = tokens.shape
    hidden = w_gate.shape[2]
    experts = lax.axis_size("expert")
    lanes = 128
    pad = ((0, 0), (0, lanes - tok_rows))
    routes_t = jnp.pad(routes.T, pad, constant_values=-1)
    codes_t = jnp.pad(gate_codes.T, pad, constant_values=1)
    vmem = pl.BlockSpec(memory_space=pltpu.VMEM)
    row_shape = jax.ShapeDtypeStruct((NZ, NY, SLOTS, width), BF16)
    dma = pltpu.SemaphoreType.DMA
    rx, rd, vx, vd, gt, flag = pl.pallas_call(
        dispatch_kernel,
        out_shape=[row_shape] * 4
        + [
            jax.ShapeDtypeStruct((NZ, experts, lanes), F32),
            jax.ShapeDtypeStruct((8, lanes), F32),
        ],
        in_specs=[vmem] * 4,
        out_specs=[vmem] * 6,
        scratch_shapes=[
            pltpu.VMEM((NZ, tok_rows, width), BF16),
            pltpu.VMEM((NZ, tok_rows, width), BF16),
            pltpu.VMEM((NZ, NY, SLOTS, width), BF16),
            pltpu.VMEM((NZ, NY, SLOTS, width), BF16),
            pltpu.VMEM((2, SLOTS, width), BF16),
            pltpu.VMEM((NZ, experts, lanes), F32),
            dma((5, NZ)),
            dma((5, NZ)),
            dma((2, NZ, NY)),
            dma((2, NZ, NY)),
            dma((2, NY)),
            dma((2, NY)),
        ],
        compiler_params=pltpu.CompilerParams(
            collective_id=0, has_side_effects=True, vmem_limit_bytes=48 << 20
        ),
        name="dispatch",
    )(tokens, out_grad, routes_t, codes_t)

    rows = NZ * NY * SLOTS
    tile = 256
    whole = pl.BlockSpec((rows, width), lambda h, f: (0, 0), pipeline_mode=pl.Buffered(1))
    columns = pl.BlockSpec((None, width, tile), lambda h, f: (0, 0, h))
    eo, ed, vo, ve, gd = pl.pallas_call(
        expert_kernel,
        out_shape=[jax.ShapeDtypeStruct((rows, width), BF16)] * 4
        + [jax.ShapeDtypeStruct((width, hidden), BF16)],
        grid_spec=pltpu.PrefetchScalarGridSpec(
            num_scalar_prefetch=1,
            grid=(hidden // tile,),
            in_specs=[whole] * 4
            + [
                columns,
                columns,
                pl.BlockSpec((None, tile, width), lambda h, f: (0, h, 0)),
            ],
            out_specs=[pl.BlockSpec((rows, width), lambda h, f: (0, 0))] * 4
            + [pl.BlockSpec((width, tile), lambda h, f: (0, h))],
            scratch_shapes=[
                pltpu.VMEM((2 * rows, width), F32),
                pltpu.VMEM((2 * rows, width), F32),
                pltpu.VMEM((width, tile), F32),
            ],
        ),
        compiler_params=pltpu.CompilerParams(
            dimension_semantics=("arbitrary",), vmem_limit_bytes=56 << 20
        ),
        name="experts",
    )(
        flag[0, :1],
        rx.reshape(rows, width),
        rd.reshape(rows, width),
        vx.reshape(rows, width),
        vd.reshape(rows, width),
        w_gate,
        w_up,
        w_down,
    )
    grad_down = lax.psum_scatter(gd, "edata", scatter_dimension=0, tiled=True)

    shape4 = (NZ, NY, SLOTS, width)
    mixed, input_grad = pl.pallas_call(
        return_kernel,
        out_shape=[jax.ShapeDtypeStruct((tok_rows, width), BF16)] * 2,
        in_specs=[vmem] * 5,
        out_specs=[vmem] * 2,
        scratch_shapes=[
            pltpu.VMEM(shape4, BF16),
            pltpu.VMEM(shape4, BF16),
            pltpu.VMEM((2, 2, NZ + 1, tok_rows, width), BF16),
            pltpu.VMEM((2, 2, NZ, tok_rows, width), BF16),
            pltpu.VMEM((2, 2, NZ + 1, NY - 1, SLOTS, width), BF16),
            pltpu.VMEM((2, 2, NZ, NY - 1, SLOTS, width), BF16),
            pltpu.VMEM((2, NY, SLOTS, width), BF16),
            pltpu.VMEM((NZ, experts, lanes), F32),
            dma((2, NZ, NY)),
            dma((2, NZ, NY)),
            dma((2, 2, 2, NZ)),
            dma((2, 2, 2, NZ + 1)),
            dma((2, NY)),
            dma((2, NY)),
        ],
        compiler_params=pltpu.CompilerParams(
            collective_id=1, has_side_effects=True, vmem_limit_bytes=56 << 20
        ),
        name="returns",
    )(
        eo.reshape(shape4), ed.reshape(shape4), vo.reshape(shape4), ve.reshape(shape4), gt
    )
    return (mixed, input_grad, grad_down.astype(F32)[:, None, :])


def solution(mesh):
    placed = (
        P(("expert", "edata"), None),
        P(("expert", "edata"), None),
        P(("expert", "edata"), None),
        P(("expert", "edata"), None),
        P("expert", None, None),
        P("expert", None, None),
        P("expert", None, None),
    )
    return jax.shard_map(
        shards,
        mesh=mesh,
        in_specs=placed,
        out_specs=(
            P(("expert", "edata"), None),
            P(("expert", "edata"), None),
            P("edata", "expert", None),
        ),
        check_vma=False,
    )
```
